32 devices in a mesh: dp: 8 (over z, y), shard: 4 (over x, core).
Axes of the slice: x: 2, y: 2, z: 4, core: 2. Of those that a mesh axis runs over, the one named last changes fastest.
Arguments:
- tokens: bfloat16 [13312, 4096], P(('dp', 'shard')), may hold values from -6 to 6
- cotangent: bfloat16 [13312, 4096], P(('dp', 'shard')), may hold values from -6 to 6
- gate_up: bfloat16 [4, 4096, 256], P('shard'), may hold values from -0.09375 to 0.09375
- down: bfloat16 [4, 128, 4096], P('shard'), may hold values from -0.09375 to 0.09375
- kept_slots: int32 [2], replicated, may hold values from 0 to 3, as said below
Outputs:
- token_grad: bfloat16 [13312, 4096], P(('dp', 'shard'))
- grad_gate_up: bfloat16 [4, 4096, 256], P('shard', 'dp')
- grad_down: bfloat16 [4, 128, 4096], P('shard', None, 'dp')
The draws below stay inside these ranges and needn't reach their ends.
Inputs may be any that keep to these rules, and one draw needn't show every extreme that they name: `kept_slots`: 2 distinct positions; position p is stored on index p // 1 of shard.
All inputs are finite; a program needn't handle non-finite values.
Results may differ from the reference program's by a relative error of at most 0.015.
Values may be sent and summed in bfloat16 or wider, within the bound.
A program may use at most 128 MiB of HBM per device.

```python
import math
import jax
import jax.numpy as jnp
from jax import lax

D = 4096
BLK = 128
KB = 2
TOK_DEV = 416
TOKENS = 13312
NB = 4
DEVICES = 32


def draw_kept_slots(key, part):
    shuffled = jax.random.permutation(jax.random.fold_in(key, 17), NB)
    return shuffled[:KB].astype(jnp.int32)


def raised(values, stream_key, source, target, shards_of, factor):
    def block_of(position):
        return (jnp.arange(values.shape[position]) // (values.shape[position] // shards_of)).reshape((-1,) + (1,) * (values.ndim - 1 - position))

    first = jax.random.permutation(stream_key, shards_of)[block_of(target)]
    second = (block_of(target) + shards_of // 2) % shards_of
    return jnp.where((block_of(source) == first) | (block_of(source) == second), factor * values, values)


def steps_of(rng, extent, shards, least, high):
    loudness = 1.0
    for position, parts in shards:
        heights = jax.random.uniform(jax.random.fold_in(jax.random.fold_in(rng, 6), position), (parts,), jnp.float32, least / len(shards), high / len(shards))
        loudness = loudness * jnp.repeat(jnp.exp(heights), extent[position] // parts).reshape((-1,) + (1,) * (len(extent) - 1 - position))
    return loudness


def bell_draw(key, extent, width, limit, pieces=(), dtype=jnp.bfloat16):
    drawn = jax.random.normal(key, extent, jnp.float32) * width
    if len(pieces) > 0:
        drawn = steps_of(key, extent, pieces, -0.22, 0.18) * drawn
    return jnp.clip(drawn, min=-limit, max=limit).astype(dtype)


def bell_draw_with(key, dims, width, reach, split, heavy, dtype=jnp.bfloat16):
    array = width * jax.random.normal(key, dims, jnp.float32)
    if split:
        array = array * steps_of(key, dims, split, -0.22, 0.18)
    return jnp.clip(raised(array, jax.random.fold_in(key, 3), *heavy), -reach, reach).astype(dtype)


def setup_inputs(seed: int = 0) -> dict:
    splits = jax.random.split(jax.random.key(seed), 6)
    return {
        "tokens": bell_draw(splits[0], (TOKENS, D), 1.0, 6.0, ((0, 32),)),
        "cotangent": bell_draw_with(splits[1], (TOKENS, D), 1.0, 6.0, ((0, 32),), (0, 1, 32, 2.75)),
        "gate_up": bell_draw(splits[2], (NB, D, 2 * BLK), D ** -0.5, 0.09375, ((0, 4),)),
        "down": bell_draw(splits[3], (NB, BLK, D), D ** -0.5, 0.09375, ((0, 4),)),
        "kept_slots": draw_kept_slots(jax.random.fold_in(splits[5], 71), 0),
    }


def device_sums(left, right):
    left_blocks = left.reshape(DEVICES, TOK_DEV, left.shape[1])
    right_blocks = right.reshape(DEVICES, TOK_DEV, right.shape[1])

    def add_one(carry, pair):
        term = lax.dot_general(pair[0], pair[1], (((0,), (0,)), ((), ())), preferred_element_type=jnp.float32)
        return (carry + term.astype(jnp.bfloat16).astype(jnp.float32), None)
    start = jnp.zeros((left.shape[1], right.shape[1]), jnp.float32)
    total, _ = lax.scan(add_one, start, (left_blocks, right_blocks))
    return total

def reference(tokens, cotangent, gate_up, down, kept_slots):
    scale_factor = 1.0 / math.sqrt(TOKENS)
    dx_total = jnp.zeros(tokens.shape, jnp.float32)
    grad_pair = jnp.zeros(gate_up.shape, jnp.float32)
    grad_back = jnp.zeros(down.shape, jnp.float32)
    for kept_pos in range(KB):
        slot_id = kept_slots[kept_pos].astype(jnp.int32)
        w_pair = lax.dynamic_index_in_dim(gate_up, slot_id, 0, keepdims=False)
        w_back = lax.dynamic_index_in_dim(down, slot_id, 0, keepdims=False)
        projected = jnp.dot(tokens, w_pair, preferred_element_type=jnp.float32)
        gate_pre = projected[:, :BLK]
        up_pre = projected[:, BLK:]
        sigmoid_gate = jax.nn.sigmoid(gate_pre)
        silu_gate = gate_pre * sigmoid_gate
        activated = (silu_gate * up_pre).astype(jnp.bfloat16)
        d_act = lax.dot_general(cotangent, w_back, (((1,), (1,)), ((), ())), preferred_element_type=jnp.float32)
        d_gate = d_act * up_pre * sigmoid_gate * (1.0 + gate_pre * (1.0 - sigmoid_gate))
        d_up = d_act * silu_gate
        d_projected = jnp.concatenate([d_gate, d_up], axis=1).astype(jnp.bfloat16)
        dx_total = dx_total + lax.dot_general(d_projected, w_pair, (((1,), (1,)), ((), ())), preferred_element_type=jnp.float32)
        term_pair = device_sums(tokens, d_projected)
        term_back = device_sums(activated, cotangent)
        grad_pair = lax.dynamic_update_index_in_dim(grad_pair, term_pair, slot_id, 0)
        grad_back = lax.dynamic_update_index_in_dim(grad_back, term_back, slot_id, 0)
    return (dx_total.astype(jnp.bfloat16), (grad_pair * scale_factor).astype(jnp.bfloat16), (grad_back * scale_factor).astype(jnp.bfloat16))
```

```python
import functools
import math

import jax
import jax.numpy as jnp
from jax import lax
from jax.experimental import pallas as pl
from jax.experimental.pallas import tpu as pltpu
from jax.sharding import PartitionSpec as P

MESH = pl.DeviceIdType.MESH
F32 = jnp.float32
BF16 = jnp.bfloat16
ALL = slice(None)


def fused(
    Z, Y, X, scale,
    kept, packed, tokens_hbm, cot_hbm,
    dx_hbm, gate_up_out, down_out,
    tok, cot, dxb, recv, sel, W, G, dproj, act, acc,
    r1, r2e, r2o, r3e, r3o, r4, fin,
    load_sem, own_sem, dx_sem, a2a_s, a2a_r, ag_s, ag_r, rs_s, rs_r, bc_s, bc_r,
):
    S = X * 2
    KB3 = W.shape[0]
    KB = KB3 // 3
    R = W.shape[-2]
    BLK = W.shape[-1]
    tile = Y * X * 2 * R
    d = lax.axis_index("dp")
    s = lax.axis_index("shard")
    me = {"z": d // Y, "y": d % Y, "x": s // 2, "c": s % 2}
    size = {"z": Z, "y": Y, "x": X, "c": 2}
    base = {"z": 0, "y": Z - 1, "x": Z - 1 + Y - 1, "c": Z - 1 + Y - 1 + X - 1}

    def device(co):
        return (co["z"] * Y + co["y"], co["x"] * 2 + co["c"])

    def peer(dim, o):
        co = dict(me)
        co[dim] = lax.rem(me[dim] + o, size[dim])
        return co

    def shard_peer(o):
        return lax.rem(s + o, S)

    load_tok = pltpu.make_async_copy(tokens_hbm, tok, load_sem.at[0])
    load_cot = pltpu.make_async_copy(cot_hbm, cot, load_sem.at[1])
    own = pltpu.make_async_copy(packed.at[:, d, s], recv.at[s], own_sem.at[0])
    own.start()

    barrier = pltpu.get_barrier_semaphore()
    greeted = [(d, shard_peer(o)) for o in range(1, S)]
    for dim in ("z", "y"):
        greeted += [device(peer(dim, o)) for o in range(1, size[dim])]
    for who in greeted:
        pl.semaphore_signal(barrier, inc=1, device_id=who, device_id_type=MESH)
    pl.semaphore_wait(barrier, len(greeted))

    a2a = []
    for o in range(1, S):
        to = shard_peer(o)
        a2a.append(pltpu.make_async_remote_copy(
            src_ref=packed.at[:, d, to], dst_ref=recv.at[s],
            send_sem=a2a_s.at[o - 1], recv_sem=a2a_r.at[o - 1],
            device_id=(d, to), device_id_type=MESH))
    for copy in a2a:
        copy.start()
    load_tok.start()
    load_cot.start()
    own.wait()
    for copy in a2a:
        copy.wait_recv()
    for k in range(KB):
        W[3 * k:3 * k + 3, me["z"], me["y"], me["x"], me["c"]] = recv[kept[k]]

    def gather_order(ch):
        return ("z", "y", "x", "c") if ch % 2 == 0 else ("z", "x", "y", "c")

    def gather_copies(ch, i):
        order = gather_order(ch)
        region = W.at[(ch,) + tuple(
            ALL if t in order[:i] else me[t] for t in ("z", "y", "x", "c"))]
        dim = order[i]
        return [pltpu.make_async_remote_copy(
            src_ref=region, dst_ref=region,
            send_sem=ag_s.at[ch, base[dim] + o - 1], recv_sem=ag_r.at[ch, base[dim] + o - 1],
            device_id=device(peer(dim, o)), device_id_type=MESH)
            for o in range(1, size[dim])]

    def gather_start(ch, i):
        for copy in gather_copies(ch, i):
            copy.start()

    def gather_wait(ch, i):
        for copy in gather_copies(ch, i):
            copy.wait_recv()

    for ch in range(KB3):
        gather_start(ch, 0)
    for i in range(3):
        for ch in range(KB3):
            gather_wait(ch, i)
            gather_start(ch, i + 1)

    def cols(z):
        return pl.ds(pl.multiple_of(z * tile, 128), tile)

    def w_tile(ch, z):
        return W[ch, z].reshape(tile, BLK)

    def pair_tile(k, z):
        return jnp.concatenate([w_tile(3 * k, z), w_tile(3 * k + 1, z)], axis=1)

    def forward(k):
        acc[...] = jnp.zeros_like(acc)

        @pl.loop(0, Z)
        def _(z):
            acc[:, :2 * BLK] += jnp.dot(tok[:, cols(z)], pair_tile(k, z), preferred_element_type=F32)
            acc[:, 2 * BLK:] += jnp.dot(cot[:, cols(z)], w_tile(3 * k + 2, z), preferred_element_type=F32)

        gate = acc[:, :BLK]
        up = acc[:, BLK:2 * BLK]
        d_act = acc[:, 2 * BLK:]
        sig = jax.nn.sigmoid(gate)
        silu = gate * sig
        act[k] = (silu * up).astype(BF16)
        dproj[k, :, :BLK] = (d_act * up * sig * (1.0 + gate * (1.0 - sig))).astype(BF16)
        dproj[k, :, BLK:] = (d_act * silu).astype(BF16)

    def grads(k):
        @pl.loop(0, Z)
        def _(z):
            pair = lax.dot_general(tok[:, cols(z)], dproj[k], (((0,), (0,)), ((), ())),
                                   preferred_element_type=F32).astype(BF16)
            G[3 * k, z] = pair[:, :BLK].reshape(Y, X, 2, R, BLK)
            G[3 * k + 1, z] = pair[:, BLK:].reshape(Y, X, 2, R, BLK)
            back = lax.dot_general(cot[:, cols(z)], act[k], (((0,), (0,)), ((), ())),
                                   preferred_element_type=F32).astype(BF16)
            G[3 * k + 2, z] = back.reshape(Y, X, 2, R, BLK)

    def dx_tile(z):
        total = jnp.zeros((tok.shape[0], tile), F32)
        for k in range(KB):
            total += lax.dot_general(dproj[k], pair_tile(k, z), (((1,), (1,)), ((), ())),
                                     preferred_element_type=F32)
        dxb[:, z * tile:(z + 1) * tile] = total.astype(BF16)
        dx_copy(z).start()

    def dx_copy(z):
        part = pl.ds(z * tile, tile)
        return pltpu.make_async_copy(dxb.at[:, part], dx_hbm.at[:, part], dx_sem.at[z])

    def scatter_order(ch):
        return ("c", "x", "y", "z") if ch % 2 == 0 else ("c", "y", "x", "z")

    def scatter_copies(ch, i):
        dim = scatter_order(ch)[i]
        h = ch // 2
        r2, r3 = (r2e, r3e) if ch % 2 == 0 else (r2o, r3o)
        out = []
        for o in range(1, size[dim]):
            to = peer(dim, o)
            at = to[dim]
            if i == 0:
                src, dst = G.at[ch, :, :, :, at], r1.at[ch]
            elif i == 1:
                src = r1.at[ch, :, :, at] if dim == "x" else r1.at[ch, :, at]
                dst = r2.at[h, o - 1]
            elif i == 2:
                src, dst = r2.at[h, 0, :, at], r3.at[h, o - 1]
            else:
                src, dst = r3.at[h, 0, at], r4.at[ch, o - 1]
            out.append(pltpu.make_async_remote_copy(
                src_ref=src, dst_ref=dst,
                send_sem=rs_s.at[ch, base[dim] + o - 1], recv_sem=rs_r.at[ch, base[dim] + o - 1],
                device_id=device(to), device_id_type=MESH))
        return out

    def scatter_start(ch, i):
        for copy in scatter_copies(ch, i):
            copy.start()

    def scatter_add(ch, i):
        for copy in scatter_copies(ch, i):
            copy.wait_recv()
        h = ch // 2
        r2, r3 = (r2e, r3e) if ch % 2 == 0 else (r2o, r3o)
        dim = scatter_order(ch)[i]
        at = me[dim]
        if i == 3:
            total = r3[h, 0, at].astype(F32)
            for o in range(1, Z):
                total += r4[ch, o - 1].astype(F32)
            fin[s, ch] = (total * scale).astype(BF16)
            return

        @pl.loop(0, Z)
        def _(z):
            if i == 0:
                r1[ch, z] = (G[ch, z, :, :, at].astype(F32) + r1[ch, z].astype(F32)).astype(BF16)
            elif i == 1:
                mine = r1[ch, z, :, at] if dim == "x" else r1[ch, z, at]
                total = mine.astype(F32)
                for o in range(1, size[dim]):
                    total += r2[h, o - 1, z].astype(F32)
                r2[h, 0, z] = total.astype(BF16)
            else:
                total = r2[h, 0, z, at].astype(F32)
                for o in range(1, size[dim]):
                    total += r3[h, o - 1, z].astype(F32)
                r3[h, 0, z] = total.astype(BF16)

    def last_copies(k):
        return [pltpu.make_async_remote_copy(
            src_ref=fin.at[s, pl.ds(3 * k, 3)], dst_ref=fin.at[s, pl.ds(3 * k, 3)],
            send_sem=bc_s.at[k, o - 1], recv_sem=bc_r.at[k, o - 1],
            device_id=(d, shard_peer(o)), device_id_type=MESH) for o in range(1, S)]

    load_tok.wait()
    load_cot.wait()
    for k in range(KB):
        for ch in range(3 * k, 3 * k + 3):
            gather_wait(ch, 3)
        forward(k)
        grads(k)
        for ch in range(3 * k, 3 * k + 3):
            scatter_start(ch, 0)
        if k > 0:
            for ch in range(3 * k - 3, 3 * k):
                scatter_add(ch, 0)
                scatter_start(ch, 1)
    for ch in range(KB3 - 3, KB3):
        scatter_add(ch, 0)
        scatter_start(ch, 1)
    half = Z // 2
    for z in range(half):
        dx_tile(z)
    for ch in range(KB3):
        scatter_add(ch, 1)
        scatter_start(ch, 2)
    for z in range(half, Z):
        dx_tile(z)
    for ch in range(KB3):
        scatter_add(ch, 2)
        scatter_start(ch, 3)
    for k in range(KB):
        for ch in range(3 * k, 3 * k + 3):
            scatter_add(ch, 3)
        for copy in last_copies(k):
            copy.start()
    for k in range(KB):
        for copy in last_copies(k):
            copy.wait_recv()

    for j in range(3):
        total = jnp.zeros((S * R, BLK), F32)
        for k in range(KB):
            hit = (kept[k] == s).astype(F32)
            total += hit * fin[:, 3 * k + j].reshape(S * R, BLK).astype(F32)
        if j < 2:
            gate_up_out[0, :, j * BLK:(j + 1) * BLK] = total.astype(BF16)
        else:
            down_out[0] = total.T.astype(BF16)

    for copy in a2a:
        copy.wait_send()
    for ch in range(KB3):
        for i in range(4):
            for copy in gather_copies(ch, i) + scatter_copies(ch, i):
                copy.wait_send()
    for k in range(KB):
        for copy in last_copies(k):
            copy.wait_send()
    for z in range(Z):
        dx_copy(z).wait()


def body(dp, shard, tokens, cotangent, gate_up, down, kept_slots):
    T, D = tokens.shape
    BLK = down.shape[1]
    KB = kept_slots.shape[0]
    Z = 4
    Y = dp // Z
    X = shard // 2
    S = shard
    R = D // (dp * shard)
    scale = 1.0 / math.sqrt(T * dp * shard)
    packed = jnp.stack([gate_up[0, :, :BLK], gate_up[0, :, BLK:], down[0].T])
    packed = packed.reshape(3, dp, shard, R, BLK)
    C = 3 * KB
    H = (C + 1) // 2
    L = (Z - 1) + (Y - 1) + (X - 1) + 1
    rows = D // dp
    vmem = pl.BlockSpec(memory_space=pltpu.VMEM)
    anym = pl.BlockSpec(memory_space=pl.ANY)
    V = pltpu.VMEM
    dma = pltpu.SemaphoreType.DMA
    return pl.pallas_call(
        functools.partial(fused, Z, Y, X, scale),
        out_shape=(
            jax.ShapeDtypeStruct((T, D), BF16),
            jax.ShapeDtypeStruct((1, rows, 2 * BLK), BF16),
            jax.ShapeDtypeStruct((1, BLK, rows), BF16),
        ),
        in_specs=[pl.BlockSpec(memory_space=pltpu.SMEM), anym, anym, anym],
        out_specs=(anym, vmem, vmem),
        scratch_shapes=[
            V((T, D), BF16), V((T, D), BF16), V((T, D), BF16),
            V((S, 3, R, BLK), BF16), V((8, 128), BF16),
            V((C, Z, Y, X, 2, R, BLK), BF16), V((C, Z, Y, X, 2, R, BLK), BF16),
            V((KB, T, 2 * BLK), BF16), V((KB, T, BLK), BF16), V((T, 3 * BLK), F32),
            V((C, Z, Y, X, R, BLK), BF16),
            V((H, X - 1, Z, Y, R, BLK), BF16), V((H, Y - 1, Z, X, R, BLK), BF16),
            V((H, Y - 1, Z, R, BLK), BF16), V((H, X - 1, Z, R, BLK), BF16),
            V((C, Z - 1, R, BLK), BF16), V((S, C, R, BLK), BF16),
            dma((2,)), dma((1,)), dma((Z,)), dma((S - 1,)), dma((S - 1,)),
            dma((C, L)), dma((C, L)), dma((C, L)), dma((C, L)),
            dma((KB, S - 1)), dma((KB, S - 1)),
        ],
        compiler_params=pltpu.CompilerParams(
            collective_id=0, has_side_effects=True, vmem_limit_bytes=58 * 1024 * 1024),
        name="fused_backward",
    )(kept_slots, packed, tokens, cotangent)


def solution(mesh):
    in_specs = (
        P(("dp", "shard"), None),
        P(("dp", "shard"), None),
        P("shard", None, None),
        P("shard", None, None),
        P(),
    )
    out_specs = (P(("dp", "shard"), None), P("shard", "dp", None), P("shard", None, "dp"))
    fn = functools.partial(body, mesh.shape["dp"], mesh.shape["shard"])
    return jax.shard_map(fn, mesh=mesh, in_specs=in_specs, out_specs=out_specs, check_vma=False)
```

```python
import functools
import math

import jax
import jax.numpy as jnp
from jax import lax
from jax.experimental import pallas as pl
from jax.experimental.pallas import tpu as pltpu
from jax.sharding import PartitionSpec as P

MESH = pl.DeviceIdType.MESH
F32 = jnp.float32
BF16 = jnp.bfloat16
ALL = slice(None)


def fused(
    Z, Y, X, scale,
    kept, pair_hbm, back_hbm, tokens_hbm, cot_hbm,
    dx_hbm, gate_up_out, down_out,
    tok, cot, dxb, recv_pair, recv_back, W, G, dproj, act, acc,
    r1, r2e, r2o, r3e, r3o, rz, r4, fin,
    load_sem, own_sem, dx_sem, a2a_s, a2a_r, ag_s, ag_r, rs_s, rs_r, bc_s, bc_r,
):
    S = X * 2
    KB3 = W.shape[0]
    KB = KB3 // 3
    R = W.shape[-2]
    BLK = W.shape[-1]
    tile = Y * X * 2 * R
    d = lax.axis_index("dp")
    s = lax.axis_index("shard")
    me = {"z": d // Y, "y": d % Y, "x": s // 2, "c": s % 2}
    size = {"z": Z, "y": Y, "x": X, "c": 2}
    hz = Z // 2
    base = {("z", 0): 0, ("c", 0): Z - 1}
    base["y", 0] = Z
    base["y", 1] = base["y", 0] + Y - 1
    base["x", 0] = base["y", 1] + Y - 1
    base["x", 1] = base["x", 0] + X - 1
    flipped = len(back_hbm.shape) == 2

    def device(co):
        return (co["z"] * Y + co["y"], co["x"] * 2 + co["c"])

    def peer(dim, o):
        co = dict(me)
        co[dim] = lax.rem(me[dim] + o, size[dim])
        return co

    def shard_peer(o):
        return lax.rem(s + o, S)

    load_tok = pltpu.make_async_copy(tokens_hbm, tok, load_sem.at[0])
    load_cot = pltpu.make_async_copy(cot_hbm, cot, load_sem.at[1])

    def pieces(who):
        row = pl.multiple_of((d * S + who) * R, R)
        if flipped:
            return (pair_hbm.at[0, pl.ds(row, R)], back_hbm.at[:, pl.ds(row, R)])
        return (pair_hbm.at[0, pl.ds(row, R)], back_hbm.at[0, pl.ds(row, R)])

    landing = (recv_pair.at[s], recv_back.at[s])
    own = [pltpu.make_async_copy(pieces(s)[p], landing[p], own_sem.at[p]) for p in range(2)]
    for copy in own:
        copy.start()

    barrier = pltpu.get_barrier_semaphore()
    greeted = [(d, shard_peer(o)) for o in range(1, S)]
    for dim in ("z", "y"):
        greeted += [device(peer(dim, o)) for o in range(1, size[dim])]
    for who in greeted:
        pl.semaphore_signal(barrier, inc=1, device_id=who, device_id_type=MESH)
    pl.semaphore_wait(barrier, len(greeted))

    a2a = []
    for o in range(1, S):
        to = shard_peer(o)
        for p in range(2):
            a2a.append(pltpu.make_async_remote_copy(
                src_ref=pieces(to)[p], dst_ref=landing[p],
                send_sem=a2a_s.at[p, o - 1], recv_sem=a2a_r.at[p, o - 1],
                device_id=(d, to), device_id_type=MESH))
    for copy in a2a:
        copy.start()
    load_tok.start()
    load_cot.start()
    for copy in own:
        copy.wait()
    for copy in a2a:
        copy.wait_recv()
    for k in range(KB):
        at = (me["z"], me["y"], me["x"], me["c"])
        pair = recv_pair[kept[k]]
        back = recv_back[kept[k]]
        if flipped:
            back = back.astype(F32).T.astype(BF16)
        W[(3 * k,) + at] = pair[:, :BLK]
        W[(3 * k + 1,) + at] = pair[:, BLK:]
        W[(3 * k + 2,) + at] = back

    def gather_copies(ch, i):
        if i == 0:
            moves = [("z", 0, (me["z"], me["y"], me["x"], me["c"]))]
        elif i == 3:
            moves = [("c", 0, (ALL, ALL, ALL, me["c"]))]
        else:
            moves = []
            for h in range(2):
                first = "yx"[h]
                dim = first if i == 1 else "xy"[h]
                y = ALL if i == 2 and first == "y" else me["y"]
                x = ALL if i == 2 and first == "x" else me["x"]
                moves.append((dim, h, (pl.ds(h * hz, hz), y, x, me["c"])))
        out = []
        for dim, h, at in moves:
            region = W.at[(ch,) + at]
            for o in range(1, size[dim]):
                n = base[dim, h] + o - 1
                out.append(pltpu.make_async_remote_copy(
                    src_ref=region, dst_ref=region,
                    send_sem=ag_s.at[ch, n], recv_sem=ag_r.at[ch, n],
                    device_id=device(peer(dim, o)), device_id_type=MESH))
        return out

    def gather_start(ch, i):
        for copy in gather_copies(ch, i):
            copy.start()

    def gather_wait(ch, i):
        for copy in gather_copies(ch, i):
            copy.wait_recv()

    def cols(z):
        return pl.ds(pl.multiple_of(z * tile, 128), tile)

    def w_tile(ch, z):
        return W[ch, z].reshape(tile, BLK)

    def pair_tile(k, z):
        return jnp.concatenate([w_tile(3 * k, z), w_tile(3 * k + 1, z)], axis=1)

    def forward(k):
        acc[...] = jnp.zeros_like(acc)

        @pl.loop(0, Z)
        def _(z):
            acc[:, :2 * BLK] += jnp.dot(tok[:, cols(z)], pair_tile(k, z), preferred_element_type=F32)
            acc[:, 2 * BLK:] += jnp.dot(cot[:, cols(z)], w_tile(3 * k + 2, z), preferred_element_type=F32)

        gate = acc[:, :BLK]
        up = acc[:, BLK:2 * BLK]
        d_act = acc[:, 2 * BLK:]
        sig = jax.nn.sigmoid(gate)
        silu = gate * sig
        act[k] = (silu * up).astype(BF16)
        dproj[k, :, :BLK] = (d_act * up * sig * (1.0 + gate * (1.0 - sig))).astype(BF16)
        dproj[k, :, BLK:] = (d_act * silu).astype(BF16)

    def grads(k):
        @pl.loop(0, Z)
        def _(z):
            pair = lax.dot_general(tok[:, cols(z)], dproj[k], (((0,), (0,)), ((), ())),
                                   preferred_element_type=F32).astype(BF16)
            G[3 * k, z] = pair[:, :BLK].reshape(Y, X, 2, R, BLK)
            G[3 * k + 1, z] = pair[:, BLK:].reshape(Y, X, 2, R, BLK)
            back = lax.dot_general(cot[:, cols(z)], act[k], (((0,), (0,)), ((), ())),
                                   preferred_element_type=F32).astype(BF16)
            G[3 * k + 2, z] = back.reshape(Y, X, 2, R, BLK)

    def dx_tile(z):
        total = jnp.zeros((tok.shape[0], tile), F32)
        for k in range(KB):
            total += lax.dot_general(dproj[k], pair_tile(k, z), (((1,), (1,)), ((), ())),
                                     preferred_element_type=F32)
        dxb[:, z * tile:(z + 1) * tile] = total.astype(BF16)
        dx_copy(z).start()

    def dx_copy(z):
        part = pl.ds(z * tile, tile)
        return pltpu.make_async_copy(dxb.at[:, part], dx_hbm.at[:, part], dx_sem.at[z])

    def scatter_moves(i):
        if i == 0:
            return [("c", 0)]
        if i == 3:
            return [("z", 0)]
        return [("xy"[h] if i == 1 else "yx"[h], h) for h in range(2)]

    def scatter_copies(ch, i):
        out = []
        for dim, h in scatter_moves(i):
            r2, r3 = ((r2e, r3e), (r2o, r3o))[h]
            zs = pl.ds(h * hz, hz)
            for o in range(1, size[dim]):
                to = peer(dim, o)
                at = to[dim]
                if i == 0:
                    src, dst = G.at[ch, :, :, :, at], r1.at[ch]
                elif i == 1:
                    src = r1.at[ch, zs, :, at] if dim == "x" else r1.at[ch, zs, at]
                    dst = r2.at[ch, o - 1]
                elif i == 2:
                    src, dst = r2.at[ch, 0, :, at], r3.at[ch, o - 1]
                else:
                    src, dst = rz.at[ch, at], r4.at[ch, o - 1]
                n = base[dim, h] + o - 1
                out.append(pltpu.make_async_remote_copy(
                    src_ref=src, dst_ref=dst,
                    send_sem=rs_s.at[ch, n], recv_sem=rs_r.at[ch, n],
                    device_id=device(to), device_id_type=MESH))
        return out

    def scatter_start(ch, i):
        for copy in scatter_copies(ch, i):
            copy.start()

    def scatter_add(ch, i):
        for copy in scatter_copies(ch, i):
            copy.wait_recv()
        if i == 3:
            total = rz[ch, me["z"]].astype(F32)
            for o in range(1, Z):
                total += r4[ch, o - 1].astype(F32)
            fin[s, ch] = (total * scale).astype(BF16)
            return
        if i == 0:
            @pl.loop(0, Z)
            def _(z):
                r1[ch, z] = (G[ch, z, :, :, me["c"]].astype(F32) + r1[ch, z].astype(F32)).astype(BF16)
            return
        for dim, h in scatter_moves(i):
            r2, r3 = ((r2e, r3e), (r2o, r3o))[h]
            at = me[dim]
            for z in range(hz):
                if i == 1:
                    zz = h * hz + z
                    mine = r1[ch, zz, :, at] if dim == "x" else r1[ch, zz, at]
                    total = mine.astype(F32)
                    for o in range(1, size[dim]):
                        total += r2[ch, o - 1, z].astype(F32)
                    r2[ch, 0, z] = total.astype(BF16)
                else:
                    total = r2[ch, 0, z, at].astype(F32)
                    for o in range(1, size[dim]):
                        total += r3[ch, o - 1, z].astype(F32)
                    rz[ch, h * hz + z] = total.astype(BF16)

    def last_copies(k):
        return [pltpu.make_async_remote_copy(
            src_ref=fin.at[s, pl.ds(3 * k, 3)], dst_ref=fin.at[s, pl.ds(3 * k, 3)],
            send_sem=bc_s.at[k, o - 1], recv_sem=bc_r.at[k, o - 1],
            device_id=(d, shard_peer(o)), device_id_type=MESH) for o in range(1, S)]

    early = range(0, 3)
    late = range(3, KB3)
    gather_start(0, 0)
    for t in range(KB3 + 3):
        for ch in range(KB3 - 1, -1, -1):
            i = t - ch
            if 0 <= i < 3:
                gather_wait(ch, i)
                if i == 0 and ch + 1 < KB3:
                    gather_start(ch + 1, 0)
                gather_start(ch, i + 1)
        if t == 5:
            load_tok.wait()
            load_cot.wait()
            for ch in early:
                gather_wait(ch, 3)
            forward(0)
        if t == 6:
            grads(0)
            for ch in early:
                scatter_start(ch, 0)
        if t == 7:
            for ch in early:
                scatter_add(ch, 0)
                scatter_start(ch, 1)
    for ch in late:
        gather_wait(ch, 3)
    for k in range(1, KB):
        forward(k)
        grads(k)
    for ch in late:
        scatter_start(ch, 0)
    for ch in early:
        scatter_add(ch, 1)
        scatter_start(ch, 2)
    for ch in late:
        scatter_add(ch, 0)
        scatter_start(ch, 1)
    half = Z // 2
    for z in range(half):
        dx_tile(z)
    for ch in early:
        scatter_add(ch, 2)
        scatter_start(ch, 3)
    for z in range(half, Z):
        dx_tile(z)
    for ch in early:
        scatter_add(ch, 3)
    for copy in last_copies(0):
        copy.start()
    for i in range(1, 3):
        for ch in late:
            scatter_add(ch, i)
            scatter_start(ch, i + 1)
    for k in range(1, KB):
        for ch in range(3 * k, 3 * k + 3):
            scatter_add(ch, 3)
        for copy in last_copies(k):
            copy.start()
    for k in range(KB):
        for copy in last_copies(k):
            copy.wait_recv()

    for j in range(3):
        total = jnp.zeros((S * R, BLK), F32)
        for k in range(KB):
            hit = (kept[k] == s).astype(F32)
            total += hit * fin[:, 3 * k + j].reshape(S * R, BLK).astype(F32)
        if j < 2:
            gate_up_out[0, :, j * BLK:(j + 1) * BLK] = total.astype(BF16)
        else:
            down_out[0] = total.T.astype(BF16)

    for copy in a2a:
        copy.wait_send()
    for ch in range(KB3):
        for i in range(4):
            for copy in gather_copies(ch, i) + scatter_copies(ch, i):
                copy.wait_send()
    for k in range(KB):
        for copy in last_copies(k):
            copy.wait_send()
    for z in range(Z):
        dx_copy(z).wait()


def body(dp, shard, tokens, cotangent, gate_up, down, kept_slots):
    T, D = tokens.shape
    BLK = down.shape[1]
    KB = kept_slots.shape[0]
    Z = 4
    Y = dp // Z
    X = shard // 2
    S = shard
    R = D // (dp * shard)
    scale = 1.0 / math.sqrt(T * dp * shard)
    if R % 128 == 0:
        back, back_piece = down[0], (BLK, R)
    else:
        back, back_piece = down[0].T[None], (R, BLK)
    C = 3 * KB
    H = Z // 2
    L = Z + 2 * (Y - 1) + 2 * (X - 1)
    rows = D // dp
    vmem = pl.BlockSpec(memory_space=pltpu.VMEM)
    anym = pl.BlockSpec(memory_space=pl.ANY)
    V = pltpu.VMEM
    dma = pltpu.SemaphoreType.DMA
    return pl.pallas_call(
        functools.partial(fused, Z, Y, X, scale),
        out_shape=(
            jax.ShapeDtypeStruct((T, D), BF16),
            jax.ShapeDtypeStruct((1, rows, 2 * BLK), BF16),
            jax.ShapeDtypeStruct((1, BLK, rows), BF16),
        ),
        in_specs=[pl.BlockSpec(memory_space=pltpu.SMEM), anym, anym, anym, anym],
        out_specs=(anym, vmem, vmem),
        scratch_shapes=[
            V((T, D), BF16), V((T, D), BF16), V((T, D), BF16),
            V((S, R, 2 * BLK), BF16), V((S,) + back_piece, BF16),
            V((C, Z, Y, X, 2, R, BLK), BF16), V((C, Z, Y, X, 2, R, BLK), BF16),
            V((KB, T, 2 * BLK), BF16), V((KB, T, BLK), BF16), V((T, 3 * BLK), F32),
            V((C, Z, Y, X, R, BLK), BF16),
            V((C, X - 1, H, Y, R, BLK), BF16), V((C, Y - 1, H, X, R, BLK), BF16),
            V((C, Y - 1, H, R, BLK), BF16), V((C, X - 1, H, R, BLK), BF16),
            V((C, Z, R, BLK), BF16),
            V((C, Z - 1, R, BLK), BF16), V((S, C, R, BLK), BF16),
            dma((2,)), dma((2,)), dma((Z,)), dma((2, S - 1)), dma((2, S - 1)),
            dma((C, L)), dma((C, L)), dma((C, L)), dma((C, L)),
            dma((KB, S - 1)), dma((KB, S - 1)),
        ],
        compiler_params=pltpu.CompilerParams(
            collective_id=0, has_side_effects=True, vmem_limit_bytes=58 * 1024 * 1024),
        name="fused_backward",
    )(kept_slots, gate_up, back, tokens, cotangent)


def solution(mesh):
    in_specs = (
        P(("dp", "shard"), None),
        P(("dp", "shard"), None),
        P("shard", None, None),
        P("shard", None, None),
        P(),
    )
    out_specs = (P(("dp", "shard"), None), P("shard", "dp", None), P("shard", None, "dp"))
    fn = functools.partial(body, mesh.shape["dp"], mesh.shape["shard"])
    return jax.shard_map(fn, mesh=mesh, in_specs=in_specs, out_specs=out_specs, check_vma=False)
```

```python
import functools
import math

import jax
import jax.numpy as jnp
from jax import lax
from jax.experimental import pallas as pl
from jax.experimental.pallas import tpu as pltpu
from jax.sharding import PartitionSpec as P

MESH = pl.DeviceIdType.MESH
F32 = jnp.float32
BF16 = jnp.bfloat16
ALL = slice(None)


def fused(
    Z, Y, X, scale,
    kept, pair_hbm, back_hbm, tokens_hbm, cot_hbm,
    dx_hbm, gate_up_out, down_out,
    tok, cot, dxb, recv_pair, recv_back, W, G, dproj, act, acc,
    r1, r2e, r2o, r3e, r3o, rz, r4, fin,
    load_sem, own_sem, dx_sem, a2a_s, a2a_r, ag_s, ag_r, rs_s, rs_r, bc_s, bc_r,
):
    S = X * 2
    KB3 = W.shape[0]
    KB = KB3 // 3
    R = W.shape[-2]
    BLK = W.shape[-1]
    tile = Y * X * 2 * R
    d = lax.axis_index("dp")
    s = lax.axis_index("shard")
    me = {"z": d // Y, "y": d % Y, "x": s // 2, "c": s % 2}
    size = {"z": Z, "y": Y, "x": X, "c": 2}
    hz = Z // 2
    base = {("z", 0): 0, ("c", 0): Z - 1}
    base["y", 0] = Z
    base["y", 1] = base["y", 0] + Y - 1
    base["x", 0] = base["y", 1] + Y - 1
    base["x", 1] = base["x", 0] + X - 1
    flipped = len(back_hbm.shape) == 2

    def device(co):
        return (co["z"] * Y + co["y"], co["x"] * 2 + co["c"])

    def peer(dim, o):
        co = dict(me)
        co[dim] = lax.rem(me[dim] + o, size[dim])
        return co

    def shard_peer(o):
        return lax.rem(s + o, S)

    load_tok = pltpu.make_async_copy(tokens_hbm, tok, load_sem.at[0])
    load_cot = pltpu.make_async_copy(cot_hbm, cot, load_sem.at[1])

    def pieces(who):
        row = pl.multiple_of((d * S + who) * R, R)
        if flipped:
            return (pair_hbm.at[0, pl.ds(row, R)], back_hbm.at[:, pl.ds(row, R)])
        return (pair_hbm.at[0, pl.ds(row, R)], back_hbm.at[0, pl.ds(row, R)])

    landing = (recv_pair.at[s], recv_back.at[s])
    own = [pltpu.make_async_copy(pieces(s)[p], landing[p], own_sem.at[p]) for p in range(2)]
    for copy in own:
        copy.start()

    barrier = pltpu.get_barrier_semaphore()
    greeted = [(d, shard_peer(o)) for o in range(1, S)]
    for dim in ("z", "y"):
        greeted += [device(peer(dim, o)) for o in range(1, size[dim])]
    for who in greeted:
        pl.semaphore_signal(barrier, inc=1, device_id=who, device_id_type=MESH)
    pl.semaphore_wait(barrier, len(greeted))

    a2a = []
    for o in range(1, S):
        to = shard_peer(o)
        for p in range(2):
            a2a.append(pltpu.make_async_remote_copy(
                src_ref=pieces(to)[p], dst_ref=landing[p],
                send_sem=a2a_s.at[p, o - 1], recv_sem=a2a_r.at[p, o - 1],
                device_id=(d, to), device_id_type=MESH))
    for copy in a2a:
        copy.start()
    load_tok.start()
    load_cot.start()
    for copy in own:
        copy.wait()
    for copy in a2a:
        copy.wait_recv()
    for k in range(KB):
        at = (me["z"], me["y"], me["x"], me["c"])
        pair = recv_pair[kept[k]]
        back = recv_back[kept[k]]
        if flipped:
            back = back.astype(F32).T.astype(BF16)
        W[(3 * k,) + at] = pair[:, :BLK]
        W[(3 * k + 1,) + at] = pair[:, BLK:]
        W[(3 * k + 2,) + at] = back

    def gather_copies(ch, i):
        if i == 0:
            moves = [("z", 0, (me["z"], me["y"], me["x"], me["c"]))]
        elif i == 3:
            moves = [("c", 0, (ALL, ALL, ALL, me["c"]))]
        else:
            moves = []
            for h in range(2):
                first = "yx"[h]
                dim = first if i == 1 else "xy"[h]
                y = ALL if i == 2 and first == "y" else me["y"]
                x = ALL if i == 2 and first == "x" else me["x"]
                moves.append((dim, h, (pl.ds(h * hz, hz), y, x, me["c"])))
        out = []
        for dim, h, at in moves:
            region = W.at[(ch,) + at]
            for o in range(1, size[dim]):
                n = base[dim, h] + o - 1
                out.append(pltpu.make_async_remote_copy(
                    src_ref=region, dst_ref=region,
                    send_sem=ag_s.at[ch, n], recv_sem=ag_r.at[ch, n],
                    device_id=device(peer(dim, o)), device_id_type=MESH))
        return out

    def gather_start(ch, i):
        for copy in gather_copies(ch, i):
            copy.start()

    def gather_wait(ch, i):
        for copy in gather_copies(ch, i):
            copy.wait_recv()

    def cols(z):
        return pl.ds(pl.multiple_of(z * tile, 128), tile)

    def w_tile(ch, z):
        return W[ch, z].reshape(tile, BLK)

    def pair_tile(k, z):
        return jnp.concatenate([w_tile(3 * k, z), w_tile(3 * k + 1, z)], axis=1)

    def forward(k):
        acc[...] = jnp.zeros_like(acc)

        @pl.loop(0, Z)
        def _(z):
            acc[:, :2 * BLK] += jnp.dot(tok[:, cols(z)], pair_tile(k, z), preferred_element_type=F32)
            acc[:, 2 * BLK:] += jnp.dot(cot[:, cols(z)], w_tile(3 * k + 2, z), preferred_element_type=F32)

        gate = acc[:, :BLK]
        up = acc[:, BLK:2 * BLK]
        d_act = acc[:, 2 * BLK:]
        sig = jax.nn.sigmoid(gate)
        silu = gate * sig
        act[k] = (silu * up).astype(BF16)
        dproj[k, :, :BLK] = (d_act * up * sig * (1.0 + gate * (1.0 - sig))).astype(BF16)
        dproj[k, :, BLK:] = (d_act * silu).astype(BF16)

    def grads(k):
        @pl.loop(0, Z)
        def _(z):
            pair = lax.dot_general(tok[:, cols(z)], dproj[k], (((0,), (0,)), ((), ())),
                                   preferred_element_type=F32).astype(BF16)
            G[3 * k, z] = pair[:, :BLK].reshape(Y, X, 2, R, BLK)
            G[3 * k + 1, z] = pair[:, BLK:].reshape(Y, X, 2, R, BLK)
            back = lax.dot_general(cot[:, cols(z)], act[k], (((0,), (0,)), ((), ())),
                                   preferred_element_type=F32).astype(BF16)
            G[3 * k + 2, z] = back.reshape(Y, X, 2, R, BLK)

    def dx_tile(z):
        total = jnp.zeros((tok.shape[0], tile), F32)
        for k in range(KB):
            total += lax.dot_general(dproj[k], pair_tile(k, z), (((1,), (1,)), ((), ())),
                                     preferred_element_type=F32)
        dxb[:, z * tile:(z + 1) * tile] = total.astype(BF16)
        dx_copy(z).start()

    def dx_copy(z):
        part = pl.ds(z * tile, tile)
        return pltpu.make_async_copy(dxb.at[:, part], dx_hbm.at[:, part], dx_sem.at[z])

    def scatter_moves(i):
        if i == 0:
            return [("c", 0)]
        if i == 3:
            return [("z", 0)]
        return [("xy"[h] if i == 1 else "yx"[h], h) for h in range(2)]

    def scatter_copies(ch, i):
        out = []
        for dim, h in scatter_moves(i):
            r2, r3 = ((r2e, r3e), (r2o, r3o))[h]
            zs = pl.ds(h * hz, hz)
            for o in range(1, size[dim]):
                to = peer(dim, o)
                at = to[dim]
                if i == 0:
                    src, dst = G.at[ch, :, :, :, at], r1.at[ch]
                elif i == 1:
                    src = r1.at[ch, zs, :, at] if dim == "x" else r1.at[ch, zs, at]
                    dst = r2.at[ch, o - 1]
                elif i == 2:
                    src, dst = r2.at[ch, 0, :, at], r3.at[ch, o - 1]
                else:
                    src, dst = rz.at[ch, at], r4.at[ch, o - 1]
                n = base[dim, h] + o - 1
                out.append(pltpu.make_async_remote_copy(
                    src_ref=src, dst_ref=dst,
                    send_sem=rs_s.at[ch, n], recv_sem=rs_r.at[ch, n],
                    device_id=device(to), device_id_type=MESH))
        return out

    def scatter_start(ch, i):
        for copy in scatter_copies(ch, i):
            copy.start()

    def scatter_add(ch, i):
        for copy in scatter_copies(ch, i):
            copy.wait_recv()
        if i == 3:
            total = rz[ch, me["z"]].astype(F32)
            for o in range(1, Z):
                total += r4[ch, o - 1].astype(F32)
            fin[s, ch] = (total * scale).astype(BF16)
            return
        if i == 0:
            @pl.loop(0, Z)
            def _(z):
                r1[ch, z] = (G[ch, z, :, :, me["c"]].astype(F32) + r1[ch, z].astype(F32)).astype(BF16)
            return
        for dim, h in scatter_moves(i):
            r2, r3 = ((r2e, r3e), (r2o, r3o))[h]
            at = me[dim]
            for z in range(hz):
                if i == 1:
                    zz = h * hz + z
                    mine = r1[ch, zz, :, at] if dim == "x" else r1[ch, zz, at]
                    total = mine.astype(F32)
                    for o in range(1, size[dim]):
                        total += r2[ch, o - 1, z].astype(F32)
                    r2[ch, 0, z] = total.astype(BF16)
                else:
                    total = r2[ch, 0, z, at].astype(F32)
                    for o in range(1, size[dim]):
                        total += r3[ch, o - 1, z].astype(F32)
                    rz[ch, h * hz + z] = total.astype(BF16)

    def last_copies(k):
        return [pltpu.make_async_remote_copy(
            src_ref=fin.at[s, pl.ds(3 * k, 3)], dst_ref=fin.at[s, pl.ds(3 * k, 3)],
            send_sem=bc_s.at[k, o - 1], recv_sem=bc_r.at[k, o - 1],
            device_id=(d, shard_peer(o)), device_id_type=MESH) for o in range(1, S)]

    early = range(0, 3)
    late = range(3, KB3)
    gather_start(0, 0)
    for t in range(KB3 + 3):
        for ch in range(KB3 - 1, -1, -1):
            i = t - ch
            if 0 <= i < 3:
                gather_wait(ch, i)
                if i == 0 and ch + 1 < KB3:
                    gather_start(ch + 1, 0)
                gather_start(ch, i + 1)
        if t == 5:
            load_tok.wait()
            load_cot.wait()
            for ch in early:
                gather_wait(ch, 3)
            forward(0)
        if t == 6:
            grads(0)
            for ch in early:
                scatter_start(ch, 0)
        if t == 7:
            for ch in early:
                scatter_add(ch, 0)
                scatter_start(ch, 1)
    for ch in late:
        gather_wait(ch, 3)
    for k in range(1, KB):
        forward(k)
        grads(k)
    for ch in late:
        scatter_start(ch, 0)
    for ch in early:
        scatter_add(ch, 1)
        scatter_start(ch, 2)
    for ch in late:
        scatter_add(ch, 0)
        scatter_start(ch, 1)
    half = Z // 2
    for z in range(half):
        dx_tile(z)
    for ch in early:
        scatter_add(ch, 2)
        scatter_start(ch, 3)
    for z in range(half, Z):
        dx_tile(z)
    for ch in early:
        scatter_add(ch, 3)
    for copy in last_copies(0):
        copy.start()
    for i in range(1, 3):
        for ch in late:
            scatter_add(ch, i)
            scatter_start(ch, i + 1)
    for k in range(1, KB):
        for ch in range(3 * k, 3 * k + 3):
            scatter_add(ch, 3)
        for copy in last_copies(k):
            copy.start()
    for k in range(KB):
        for copy in last_copies(k):
            copy.wait_recv()

    for j in range(3):
        total = jnp.zeros((S * R, BLK), F32)
        for k in range(KB):
            hit = (kept[k] == s).astype(F32)
            total += hit * fin[:, 3 * k + j].reshape(S * R, BLK).astype(F32)
        if j < 2:
            gate_up_out[0, :, j * BLK:(j + 1) * BLK] = total.astype(BF16)
        else:
            down_out[0] = total.T.astype(BF16)

    for copy in a2a:
        copy.wait_send()
    for ch in range(KB3):
        for i in range(4):
            for copy in gather_copies(ch, i) + scatter_copies(ch, i):
                copy.wait_send()
    for k in range(KB):
        for copy in last_copies(k):
            copy.wait_send()
    for z in range(Z):
        dx_copy(z).wait()


def body(dp, shard, tokens, cotangent, gate_up, down, kept_slots):
    T, D = tokens.shape
    BLK = down.shape[1]
    KB = kept_slots.shape[0]
    Z = 4
    Y = dp // Z
    X = shard // 2
    S = shard
    R = D // (dp * shard)
    scale = 1.0 / math.sqrt(T * dp * shard)
    if R % 128 == 0:
        back, back_piece = down[0], (BLK, R)
    else:
        back, back_piece = down[0].T[None], (R, BLK)
    C = 3 * KB
    H = Z // 2
    L = Z + 2 * (Y - 1) + 2 * (X - 1)
    rows = D // dp
    vmem = pl.BlockSpec(memory_space=pltpu.VMEM)
    anym = pl.BlockSpec(memory_space=pl.ANY)
    hbm = pl.BlockSpec(memory_space=pltpu.HBM)
    V = pltpu.VMEM
    dma = pltpu.SemaphoreType.DMA
    return pl.pallas_call(
        functools.partial(fused, Z, Y, X, scale),
        out_shape=(
            jax.ShapeDtypeStruct((T, D), BF16),
            jax.ShapeDtypeStruct((1, rows, 2 * BLK), BF16),
            jax.ShapeDtypeStruct((1, BLK, rows), BF16),
        ),
        in_specs=[pl.BlockSpec(memory_space=pltpu.SMEM), hbm, hbm, hbm, hbm],
        out_specs=(anym, vmem, vmem),
        scratch_shapes=[
            V((T, D), BF16), V((T, D), BF16), V((T, D), BF16),
            V((S, R, 2 * BLK), BF16), V((S,) + back_piece, BF16),
            V((C, Z, Y, X, 2, R, BLK), BF16), V((C, Z, Y, X, 2, R, BLK), BF16),
            V((KB, T, 2 * BLK), BF16), V((KB, T, BLK), BF16), V((T, 3 * BLK), F32),
            V((C, Z, Y, X, R, BLK), BF16),
            V((C, X - 1, H, Y, R, BLK), BF16), V((C, Y - 1, H, X, R, BLK), BF16),
            V((C, Y - 1, H, R, BLK), BF16), V((C, X - 1, H, R, BLK), BF16),
            V((C, Z, R, BLK), BF16),
            V((C, Z - 1, R, BLK), BF16), V((S, C, R, BLK), BF16),
            dma((2,)), dma((2,)), dma((Z,)), dma((2, S - 1)), dma((2, S - 1)),
            dma((C, L)), dma((C, L)), dma((C, L)), dma((C, L)),
            dma((KB, S - 1)), dma((KB, S - 1)),
        ],
        compiler_params=pltpu.CompilerParams(
            collective_id=0, has_side_effects=True, vmem_limit_bytes=40 * 1024 * 1024),
        name="fused_backward",
    )(kept_slots, *(pltpu.with_memory_space_constraint(v, pltpu.HBM)
                   for v in (gate_up, back, tokens, cotangent)))


def solution(mesh):
    in_specs = (
        P(("dp", "shard"), None),
        P(("dp", "shard"), None),
        P("shard", None, None),
        P("shard", None, None),
        P(),
    )
    out_specs = (P(("dp", "shard"), None), P("shard", "dp", None), P("shard", None, "dp"))
    fn = functools.partial(body, mesh.shape["dp"], mesh.shape["shard"])
    return jax.shard_map(fn, mesh=mesh, in_specs=in_specs, out_specs=out_specs, check_vma=False)
```

```python
import functools
import math

import jax
import jax.numpy as jnp
from jax import lax
from jax.experimental import pallas as pl
from jax.experimental.pallas import tpu as pltpu
from jax.sharding import PartitionSpec as P

MESH = pl.DeviceIdType.MESH
F32 = jnp.float32
BF16 = jnp.bfloat16
ALL = slice(None)


def fused(
    Z, Y, X, scale,
    kept, pair_hbm, back_hbm, tokens_hbm, cot_hbm,
    dx_hbm, gate_up_out, down_out,
    tok, cot, dxb, recv_pair, recv_back, W, G, dproj, act, acc,
    r1, r2e, r2o, r3e, r3o, rz, r4, fin,
    load_sem, own_sem, dx_sem, a2a_s, a2a_r, ag_s, ag_r, rs_s, rs_r, bc_s, bc_r,
):
    S = X * 2
    KB3 = W.shape[0]
    KB = KB3 // 3
    R = W.shape[-2]
    BLK = W.shape[-1]
    tile = Y * X * 2 * R
    d = lax.axis_index("dp")
    s = lax.axis_index("shard")
    me = {"z": d // Y, "y": d % Y, "x": s // 2, "c": s % 2}
    size = {"z": Z, "y": Y, "x": X, "c": 2}
    hz = Z // 2
    base = {("z", 0): 0, ("c", 0): Z - 1}
    base["y", 0] = Z
    base["y", 1] = base["y", 0] + Y - 1
    base["x", 0] = base["y", 1] + Y - 1
    base["x", 1] = base["x", 0] + X - 1
    flipped = len(back_hbm.shape) == 2

    def device(co):
        return (co["z"] * Y + co["y"], co["x"] * 2 + co["c"])

    def peer(dim, o):
        co = dict(me)
        co[dim] = lax.rem(me[dim] + o, size[dim])
        return co

    def shard_peer(o):
        return lax.rem(s + o, S)

    load_tok = pltpu.make_async_copy(tokens_hbm, tok, load_sem.at[0])
    load_cot = pltpu.make_async_copy(cot_hbm, cot, load_sem.at[1])

    def pieces(who):
        row = pl.multiple_of((d * S + who) * R, R)
        if flipped:
            return (pair_hbm.at[0, pl.ds(row, R)], back_hbm.at[:, pl.ds(row, R)])
        return (pair_hbm.at[0, pl.ds(row, R)], back_hbm.at[0, pl.ds(row, R)])

    landing = (recv_pair.at[s], recv_back.at[s])
    own = [pltpu.make_async_copy(pieces(s)[p], landing[p], own_sem.at[p]) for p in range(2)]
    for copy in own:
        copy.start()

    barrier = pltpu.get_barrier_semaphore()
    greeted = [(d, shard_peer(o)) for o in range(1, S)]
    for dim in ("z", "y"):
        greeted += [device(peer(dim, o)) for o in range(1, size[dim])]
    for who in greeted:
        pl.semaphore_signal(barrier, inc=1, device_id=who, device_id_type=MESH)
    pl.semaphore_wait(barrier, len(greeted))

    a2a = []
    for o in range(1, S):
        to = shard_peer(o)
        for p in range(2):
            a2a.append(pltpu.make_async_remote_copy(
                src_ref=pieces(to)[p], dst_ref=landing[p],
                send_sem=a2a_s.at[p, o - 1], recv_sem=a2a_r.at[p, o - 1],
                device_id=(d, to), device_id_type=MESH))
    for copy in a2a:
        copy.start()
    load_tok.start()
    load_cot.start()
    for copy in own:
        copy.wait()
    for copy in a2a:
        copy.wait_recv()
    for k in range(KB):
        at = (me["z"], me["y"], me["x"], me["c"])
        pair = recv_pair[kept[k]]
        back = recv_back[kept[k]]
        if flipped:
            back = back.astype(F32).T.astype(BF16)
        W[(3 * k,) + at] = pair[:, :BLK]
        W[(3 * k + 1,) + at] = pair[:, BLK:]
        W[(3 * k + 2,) + at] = back

    def gather_copies(ch, i):
        if i == 0:
            moves = [("z", 0, (me["z"], me["y"], me["x"], me["c"]))]
        elif i == 3:
            moves = [("c", 0, (ALL, ALL, ALL, me["c"]))]
        else:
            moves = []
            for h in range(2):
                first = "yx"[h]
                dim = first if i == 1 else "xy"[h]
                y = ALL if i == 2 and first == "y" else me["y"]
                x = ALL if i == 2 and first == "x" else me["x"]
                moves.append((dim, h, (pl.ds(h * hz, hz), y, x, me["c"])))
        out = []
        for dim, h, at in moves:
            region = W.at[(ch,) + at]
            for o in range(1, size[dim]):
                n = base[dim, h] + o - 1
                out.append(pltpu.make_async_remote_copy(
                    src_ref=region, dst_ref=region,
                    send_sem=ag_s.at[ch, n], recv_sem=ag_r.at[ch, n],
                    device_id=device(peer(dim, o)), device_id_type=MESH))
        return out

    def gather_start(ch, i):
        for copy in gather_copies(ch, i):
            copy.start()

    def gather_wait(ch, i):
        for copy in gather_copies(ch, i):
            copy.wait_recv()

    def cols(z):
        return pl.ds(pl.multiple_of(z * tile, 128), tile)

    def w_tile(ch, z):
        return W[ch, z].reshape(tile, BLK)

    def pair_tile(k, z):
        return jnp.concatenate([w_tile(3 * k, z), w_tile(3 * k + 1, z)], axis=1)

    def forward(k):
        acc[...] = jnp.zeros_like(acc)

        @pl.loop(0, Z)
        def _(z):
            acc[:, :2 * BLK] += jnp.dot(tok[:, cols(z)], pair_tile(k, z), preferred_element_type=F32)
            acc[:, 2 * BLK:] += jnp.dot(cot[:, cols(z)], w_tile(3 * k + 2, z), preferred_element_type=F32)

        gate = acc[:, :BLK]
        up = acc[:, BLK:2 * BLK]
        d_act = acc[:, 2 * BLK:]
        sig = jax.nn.sigmoid(gate)
        silu = gate * sig
        act[k] = (silu * up).astype(BF16)
        dproj[k, :, :BLK] = (d_act * up * sig * (1.0 + gate * (1.0 - sig))).astype(BF16)
        dproj[k, :, BLK:] = (d_act * silu).astype(BF16)

    def grads(k):
        @pl.loop(0, Z)
        def _(z):
            pair = lax.dot_general(tok[:, cols(z)], dproj[k], (((0,), (0,)), ((), ())),
                                   preferred_element_type=F32).astype(BF16)
            G[3 * k, z] = pair[:, :BLK].reshape(Y, X, 2, R, BLK)
            G[3 * k + 1, z] = pair[:, BLK:].reshape(Y, X, 2, R, BLK)
        scatter_start(3 * k, 0)
        scatter_start(3 * k + 1, 0)

        @pl.loop(0, Z)
        def _(z):
            back = lax.dot_general(cot[:, cols(z)], act[k], (((0,), (0,)), ((), ())),
                                   preferred_element_type=F32).astype(BF16)
            G[3 * k + 2, z] = back.reshape(Y, X, 2, R, BLK)

        scatter_start(3 * k + 2, 0)

    def dx_tile(z):
        total = jnp.zeros((tok.shape[0], tile), F32)
        for k in range(KB):
            total += lax.dot_general(dproj[k], pair_tile(k, z), (((1,), (1,)), ((), ())),
                                     preferred_element_type=F32)
        dxb[:, z * tile:(z + 1) * tile] = total.astype(BF16)
        dx_copy(z).start()

    def dx_copy(z):
        part = pl.ds(z * tile, tile)
        return pltpu.make_async_copy(dxb.at[:, part], dx_hbm.at[:, part], dx_sem.at[z])

    def scatter_moves(i):
        if i == 0:
            return [("c", 0)]
        if i == 3:
            return [("z", 0)]
        return [("xy"[h] if i == 1 else "yx"[h], h) for h in range(2)]

    def scatter_copies(ch, i):
        out = []
        for dim, h in scatter_moves(i):
            r2, r3 = ((r2e, r3e), (r2o, r3o))[h]
            zs = pl.ds(h * hz, hz)
            for o in range(1, size[dim]):
                to = peer(dim, o)
                at = to[dim]
                if i == 0:
                    src, dst = G.at[ch, :, :, :, at], r1.at[ch]
                elif i == 1:
                    src = r1.at[ch, zs, :, at] if dim == "x" else r1.at[ch, zs, at]
                    dst = r2.at[ch, o - 1]
                elif i == 2:
                    src, dst = r2.at[ch, 0, :, at], r3.at[ch, o - 1]
                else:
                    src, dst = rz.at[ch, at], r4.at[ch, o - 1]
                n = base[dim, h] + o - 1
                out.append(pltpu.make_async_remote_copy(
                    src_ref=src, dst_ref=dst,
                    send_sem=rs_s.at[ch, n], recv_sem=rs_r.at[ch, n],
                    device_id=device(to), device_id_type=MESH))
        return out

    def scatter_start(ch, i):
        for copy in scatter_copies(ch, i):
            copy.start()

    def scatter_add(ch, i):
        for copy in scatter_copies(ch, i):
            copy.wait_recv()
        if i == 3:
            total = rz[ch, me["z"]].astype(F32)
            for o in range(1, Z):
                total += r4[ch, o - 1].astype(F32)
            fin[s, ch] = (total * scale).astype(BF16)
            return
        if i == 0:
            @pl.loop(0, Z)
            def _(z):
                r1[ch, z] = (G[ch, z, :, :, me["c"]].astype(F32) + r1[ch, z].astype(F32)).astype(BF16)
            return
        for dim, h in scatter_moves(i):
            r2, r3 = ((r2e, r3e), (r2o, r3o))[h]
            at = me[dim]
            for z in range(hz):
                if i == 1:
                    zz = h * hz + z
                    mine = r1[ch, zz, :, at] if dim == "x" else r1[ch, zz, at]
                    total = mine.astype(F32)
                    for o in range(1, size[dim]):
                        total += r2[ch, o - 1, z].astype(F32)
                    r2[ch, 0, z] = total.astype(BF16)
                else:
                    total = r2[ch, 0, z, at].astype(F32)
                    for o in range(1, size[dim]):
                        total += r3[ch, o - 1, z].astype(F32)
                    rz[ch, h * hz + z] = total.astype(BF16)

    def last_copies(k):
        return [pltpu.make_async_remote_copy(
            src_ref=fin.at[s, pl.ds(3 * k, 3)], dst_ref=fin.at[s, pl.ds(3 * k, 3)],
            send_sem=bc_s.at[k, o - 1], recv_sem=bc_r.at[k, o - 1],
            device_id=(d, shard_peer(o)), device_id_type=MESH) for o in range(1, S)]

    early = range(0, 3)
    late = range(3, KB3)
    gather_start(0, 0)
    gather_start(1, 0)
    for t in range(KB3 + 3):
        for ch in range(KB3 - 1, -1, -1):
            i = t - ch
            if 0 <= i < 3:
                gather_wait(ch, i)
                if i == 0 and ch + 2 < KB3:
                    gather_start(ch + 2, 0)
                gather_start(ch, i + 1)
        if t == 5:
            load_tok.wait()
            load_cot.wait()
            for ch in early:
                gather_wait(ch, 3)
            forward(0)
        if t == 6:
            grads(0)
        if t == 7:
            for ch in early:
                scatter_add(ch, 0)
                scatter_start(ch, 1)
    for ch in late:
        gather_wait(ch, 3)
    for k in range(1, KB):
        forward(k)
        grads(k)
    for ch in early:
        scatter_add(ch, 1)
        scatter_start(ch, 2)
    for ch in late:
        scatter_add(ch, 0)
        scatter_start(ch, 1)
    half = Z // 2
    for z in range(half):
        dx_tile(z)
    for ch in early:
        scatter_add(ch, 2)
        scatter_start(ch, 3)
    for z in range(half, Z):
        dx_tile(z)
    for ch in early:
        scatter_add(ch, 3)
    for copy in last_copies(0):
        copy.start()
    for i in range(1, 3):
        for ch in late:
            scatter_add(ch, i)
            scatter_start(ch, i + 1)
    for k in range(1, KB):
        for ch in range(3 * k, 3 * k + 3):
            scatter_add(ch, 3)
        for copy in last_copies(k):
            copy.start()
    for k in range(KB):
        for copy in last_copies(k):
            copy.wait_recv()

    for j in range(3):
        total = jnp.zeros((S * R, BLK), F32)
        for k in range(KB):
            hit = (kept[k] == s).astype(F32)
            total += hit * fin[:, 3 * k + j].reshape(S * R, BLK).astype(F32)
        if j < 2:
            gate_up_out[0, :, j * BLK:(j + 1) * BLK] = total.astype(BF16)
        else:
            down_out[0] = total.T.astype(BF16)

    for copy in a2a:
        copy.wait_send()
    for ch in range(KB3):
        for i in range(4):
            for copy in gather_copies(ch, i) + scatter_copies(ch, i):
                copy.wait_send()
    for k in range(KB):
        for copy in last_copies(k):
            copy.wait_send()
    for z in range(Z):
        dx_copy(z).wait()


def body(dp, shard, tokens, cotangent, gate_up, down, kept_slots):
    T, D = tokens.shape
    BLK = down.shape[1]
    KB = kept_slots.shape[0]
    Z = 4
    Y = dp // Z
    X = shard // 2
    S = shard
    R = D // (dp * shard)
    scale = 1.0 / math.sqrt(T * dp * shard)
    if R % 128 == 0:
        back, back_piece = down[0], (BLK, R)
    else:
        back, back_piece = down[0].T[None], (R, BLK)
    C = 3 * KB
    H = Z // 2
    L = Z + 2 * (Y - 1) + 2 * (X - 1)
    rows = D // dp
    vmem = pl.BlockSpec(memory_space=pltpu.VMEM)
    anym = pl.BlockSpec(memory_space=pl.ANY)
    hbm = pl.BlockSpec(memory_space=pltpu.HBM)
    V = pltpu.VMEM
    dma = pltpu.SemaphoreType.DMA
    return pl.pallas_call(
        functools.partial(fused, Z, Y, X, scale),
        out_shape=(
            jax.ShapeDtypeStruct((T, D), BF16),
            jax.ShapeDtypeStruct((1, rows, 2 * BLK), BF16),
            jax.ShapeDtypeStruct((1, BLK, rows), BF16),
        ),
        in_specs=[pl.BlockSpec(memory_space=pltpu.SMEM), hbm, hbm, hbm, hbm],
        out_specs=(anym, vmem, vmem),
        scratch_shapes=[
            V((T, D), BF16), V((T, D), BF16), V((T, D), BF16),
            V((S, R, 2 * BLK), BF16), V((S,) + back_piece, BF16),
            V((C, Z, Y, X, 2, R, BLK), BF16), V((C, Z, Y, X, 2, R, BLK), BF16),
            V((KB, T, 2 * BLK), BF16), V((KB, T, BLK), BF16), V((T, 3 * BLK), F32),
            V((C, Z, Y, X, R, BLK), BF16),
            V((C, X - 1, H, Y, R, BLK), BF16), V((C, Y - 1, H, X, R, BLK), BF16),
            V((C, Y - 1, H, R, BLK), BF16), V((C, X - 1, H, R, BLK), BF16),
            V((C, Z, R, BLK), BF16),
            V((C, Z - 1, R, BLK), BF16), V((S, C, R, BLK), BF16),
            dma((2,)), dma((2,)), dma((Z,)), dma((2, S - 1)), dma((2, S - 1)),
            dma((C, L)), dma((C, L)), dma((C, L)), dma((C, L)),
            dma((KB, S - 1)), dma((KB, S - 1)),
        ],
        compiler_params=pltpu.CompilerParams(
            collective_id=0, has_side_effects=True, vmem_limit_bytes=40 * 1024 * 1024),
        name="fused_backward",
    )(kept_slots, *(pltpu.with_memory_space_constraint(v, pltpu.HBM)
                   for v in (gate_up, back, tokens, cotangent)))


def solution(mesh):
    in_specs = (
        P(("dp", "shard"), None),
        P(("dp", "shard"), None),
        P("shard", None, None),
        P("shard", None, None),
        P(),
    )
    out_specs = (P(("dp", "shard"), None), P("shard", "dp", None), P("shard", None, "dp"))
    fn = functools.partial(body, mesh.shape["dp"], mesh.shape["shard"])
    return jax.shard_map(fn, mesh=mesh, in_specs=in_specs, out_specs=out_specs, check_vma=False)
```
